128 devices in a mesh: dp: 4 (over x), fsdp: 4 (over y), ctx: 8 (over z, core).
Axes of the slice: x: 4, y: 4, z: 4, core: 2. Of those that a mesh axis runs over, the one named last changes fastest.
Arguments:
- hidden: bfloat16 [16, 2048, 8192], P(('dp', 'fsdp'), 'ctx'), may hold values from -6 to 6
- queries: bfloat16 [16, 2048, 4096], P(('dp', 'fsdp'), 'ctx'), may hold values from -40 to 40
- rotary_keys: bfloat16 [16, 2048, 512], P(('dp', 'fsdp'), 'ctx'), may hold values from -6 to 6
- attn_cotangent: bfloat16 [16, 2048, 4096], P(('dp', 'fsdp'), 'ctx'), may hold values from -6 to 6
- value_matrix: bfloat16 [8192, 512], P(('fsdp', 'ctx')), may hold values from -0.0625 to 0.0625
- keep_index: int32 [16, 1024], P(('dp', 'fsdp')), may hold values from 0 to 2047, as said below
Outputs:
- attn: bfloat16 [16, 2048, 4096], P(('dp', 'fsdp'), 'ctx')
- grad_hidden: bfloat16 [16, 2048, 8192], P(('dp', 'fsdp'), 'ctx')
- grad_queries: bfloat16 [16, 2048, 4096], P(('dp', 'fsdp'), 'ctx')
- grad_keys: bfloat16 [16, 2048, 512], P(('dp', 'fsdp'), 'ctx')
- grad_weight: bfloat16 [8192, 512], P(('fsdp', 'ctx'))
The draws below stay inside these ranges and needn't reach their ends.
Inputs may be any that keep to these rules, and one draw needn't show every extreme that they name: `keep_index`: each row lists 1024 distinct positions of its sequence in ascending order. For every c, the number of listed positions below c * 256 lies within 32 of c * 128, and in every row it exceeds c * 128 by exactly 32 for some c.
All inputs are finite; a program needn't handle non-finite values.
Results may differ from the reference program's by a relative error of at most 0.018.
Values may be sent and summed in bfloat16 or wider, within the bound.
No kernel may reach another device: no remote copies, remote signals or barrier semaphores. Data moves between devices by JAX's collectives and lax.ppermute only.
A program may use at most 256 MiB of HBM per device.

```python
import math
from functools import partial
import jax
import jax.numpy as jnp
from jax import lax

MODEL_WIDTH = 8192
HEAD_SIZE = 128
QUERY_HEADS = 32
KEY_VALUE_HEADS = 4
TOK_DEV = 256
BAL = 128
HALF = 32
SEQUENCE_LENGTH = 2048
KEEP = 1024
SEQUENCE_COUNT = 16
N_CTX = 8


def draw_keep_index(key, part):

    def one_list(seq_key):
        drift_seed, peak_seed, order_seed = jax.random.split(seq_key, 3)
        drift = jax.random.randint(drift_seed, (N_CTX + 1,), -HALF, HALF + 1)
        peak_at = jax.random.randint(peak_seed, (), 1, max(N_CTX, 2))
        drift = drift.at[peak_at].set(HALF)
        drift = drift.at[0].set(0).at[N_CTX].set(0)
        edges = jnp.arange(N_CTX + 1, dtype=jnp.int32) * BAL + drift
        counts_each = edges[1:] - edges[:-1]

        def shard_order(shard_seed):
            return jax.random.permutation(shard_seed, TOK_DEV)
        ranking = jax.vmap(shard_order)(jax.random.split(order_seed, N_CTX))
        chosen = (ranking < counts_each[:, None]).reshape(-1)
        position_ids = jnp.arange(SEQUENCE_LENGTH, dtype=jnp.int32)
        ordering = jnp.where(chosen, 0, SEQUENCE_LENGTH) + position_ids
        return jnp.argsort(ordering)[:KEEP].astype(jnp.int32)
    return jax.vmap(one_list)(jax.random.split(key, SEQUENCE_COUNT))


def query_key_pair(key):
    base_seed = jax.random.fold_in(key, 11)
    query_random_seed, key_random_seed = jax.random.split(base_seed, 2)
    heads_per_group = QUERY_HEADS // KEY_VALUE_HEADS
    query_sample = jnp.clip(jax.random.normal(query_random_seed, (SEQUENCE_COUNT, SEQUENCE_LENGTH, KEY_VALUE_HEADS, heads_per_group, HEAD_SIZE)), -6.0, 6.0)
    key_sample = jnp.clip(jax.random.normal(key_random_seed, (SEQUENCE_COUNT, SEQUENCE_LENGTH, KEY_VALUE_HEADS, HEAD_SIZE)), -6.0, 6.0)
    return (query_sample.reshape(SEQUENCE_COUNT, SEQUENCE_LENGTH, QUERY_HEADS * HEAD_SIZE), key_sample.reshape(SEQUENCE_COUNT, SEQUENCE_LENGTH, KEY_VALUE_HEADS * HEAD_SIZE))


def draw_queries(key, part):
    return query_key_pair(key)[0].astype(jnp.bfloat16)


def draw_rotary_keys(key, part):
    return query_key_pair(key)[1].astype(jnp.bfloat16)


def spiked(values, key, source, target, parts, factor):
    def block_of(position):
        return (jnp.arange(values.shape[position]) // (values.shape[position] // parts)).reshape((-1,) + (1,) * (values.ndim - 1 - position))

    near = jax.random.permutation(key, parts)[block_of(target)]
    second = (block_of(target) + parts // 2) % parts
    return jnp.where((block_of(source) == near) | (block_of(source) == second), factor * values, values)


def levels(stream_key, dims, cuts, smallest, top_value):
    def one(axis_at, blocks):
        heights = jax.random.uniform(jax.random.fold_in(jax.random.fold_in(stream_key, 6), axis_at), (blocks,), jnp.float32, smallest / len(cuts), top_value / len(cuts))
        return jnp.repeat(jnp.exp(heights), dims[axis_at] // blocks).reshape((-1,) + (1,) * (len(dims) - axis_at - 1))

    level = one(*cuts[0])
    for cut in cuts[1:]:
        level = level * one(*cut)
    return level


def noise(own_key, shape, scale, bound, shards=(), kind=jnp.bfloat16):
    entries = scale * jax.random.normal(own_key, shape, jnp.float32)
    if shards:
        entries = entries * levels(own_key, shape, shards, -0.22, 0.18)
    return jnp.clip(entries, -bound, bound).astype(kind)


def heavy_noise(stream_key, dims, scale, limit, shards, heavy, kind=jnp.bfloat16):
    entries = scale * jax.random.normal(stream_key, dims, jnp.float32)
    if shards:
        entries = entries * levels(stream_key, dims, shards, -0.22, 0.18)
    return jnp.clip(spiked(entries, jax.random.fold_in(stream_key, 3), *heavy), -limit, limit).astype(kind)


def setup_inputs(seed: int = 0) -> dict:
    key_of = jax.random.split(jax.random.key(seed), 7)
    hidden = heavy_noise(key_of[0], (SEQUENCE_COUNT, SEQUENCE_LENGTH, MODEL_WIDTH), 1.0, 6.0, ((0, 16), (1, 8)), (1, 2, 8, 2.0))
    queries = draw_queries(jax.random.fold_in(key_of[6], 71), 0)
    rotary_keys = draw_rotary_keys(jax.random.fold_in(key_of[6], 71), 0)
    attn_cotangent = noise(key_of[3], (SEQUENCE_COUNT, SEQUENCE_LENGTH, QUERY_HEADS * HEAD_SIZE), 1.0, 6.0, ((0, 16), (1, 8)))
    value_matrix = noise(key_of[4], (MODEL_WIDTH, KEY_VALUE_HEADS * HEAD_SIZE), MODEL_WIDTH ** -0.5, 0.0625, ((0, 32),))
    keep_index = draw_keep_index(jax.random.fold_in(key_of[6], 71), 0)
    return dict(hidden=hidden, queries=queries, rotary_keys=rotary_keys, attn_cotangent=attn_cotangent, value_matrix=value_matrix, keep_index=keep_index)


def attend_group(kv_group, allowed, score_scale):
    query_part, key_part, value_part, cot_part = kv_group
    query_wide = query_part.astype(jnp.float32)
    key_wide = key_part.astype(jnp.float32)
    value_wide = value_part.astype(jnp.float32)
    cot_wide = cot_part.astype(jnp.float32)
    scores = jnp.einsum('rjd,td->jrt', query_wide, key_wide) * score_scale
    scores = jnp.where(allowed[None], scores, -1e+30)
    row_max = lax.optimization_barrier(jnp.max(scores, axis=2, keepdims=True))
    weights = jnp.where(allowed[None], jnp.exp(scores - row_max), 0.0)
    softmax_probs = (weights / lax.optimization_barrier(jnp.sum(weights, axis=2, keepdims=True))).astype(jnp.bfloat16)
    probs_wide = softmax_probs.astype(jnp.float32)
    attended = jnp.einsum('jrt,td->rjd', probs_wide, value_wide).astype(jnp.bfloat16)
    row_dot = lax.optimization_barrier(jnp.sum(cot_wide * attended.astype(jnp.float32), axis=2))
    dprobs = jnp.einsum('rjd,td->jrt', cot_wide, value_wide)
    grad_scores = (probs_wide * (dprobs - jnp.transpose(row_dot)[:, :, None])).astype(jnp.bfloat16)
    scores_wide = grad_scores.astype(jnp.float32)
    grad_query = (jnp.einsum('jrt,td->rjd', scores_wide, key_wide) * score_scale).astype(jnp.bfloat16)
    key_gradient = (jnp.einsum('jrt,rjd->td', scores_wide, query_wide) * score_scale).astype(jnp.bfloat16)
    value_gradient = jnp.einsum('jrt,rjd->td', probs_wide, cot_wide).astype(jnp.bfloat16)
    return (attended, grad_query, key_gradient, value_gradient)

def one_sequence(seq_hidden, seq_queries, seq_keys, seq_cot, value_matrix, kept_list):
    retained_count = kept_list.shape[0]
    heads_per_group = QUERY_HEADS // KEY_VALUE_HEADS
    kept_hidden = jnp.take(seq_hidden, kept_list, axis=0)
    retained_queries = jnp.take(seq_queries, kept_list, axis=0)
    retained_keys = jnp.take(seq_keys, kept_list, axis=0)
    retained_cotangent = jnp.take(seq_cot, kept_list, axis=0)
    retained_values = jnp.dot(kept_hidden, value_matrix, preferred_element_type=jnp.float32).astype(jnp.bfloat16)
    order_ids = jnp.arange(retained_count, dtype=jnp.int32)
    allowed = order_ids[None, :] <= order_ids[:, None]
    grouped_result = (jnp.moveaxis(retained_queries.reshape(retained_count, KEY_VALUE_HEADS, heads_per_group, HEAD_SIZE), 1, 0), jnp.moveaxis(retained_keys.reshape(retained_count, KEY_VALUE_HEADS, HEAD_SIZE), 1, 0), jnp.moveaxis(retained_values.reshape(retained_count, KEY_VALUE_HEADS, HEAD_SIZE), 1, 0), jnp.moveaxis(retained_cotangent.reshape(retained_count, KEY_VALUE_HEADS, heads_per_group, HEAD_SIZE), 1, 0))
    attended, grad_query, key_gradient, value_gradient = lax.map(partial(attend_group, allowed=allowed, score_scale=1.0 / math.sqrt(HEAD_SIZE)), grouped_result)
    attended = jnp.moveaxis(attended, 0, 1).reshape(retained_count, QUERY_HEADS * HEAD_SIZE)
    grad_query = jnp.moveaxis(grad_query, 0, 1).reshape(retained_count, QUERY_HEADS * HEAD_SIZE)
    key_gradient = jnp.moveaxis(key_gradient, 0, 1).reshape(retained_count, KEY_VALUE_HEADS * HEAD_SIZE)
    value_gradient = jnp.moveaxis(value_gradient, 0, 1).reshape(retained_count, KEY_VALUE_HEADS * HEAD_SIZE)
    grad_rows = jnp.dot(value_gradient, jnp.transpose(value_matrix), preferred_element_type=jnp.float32).astype(jnp.bfloat16)
    weight_term = jnp.dot(jnp.transpose(kept_hidden), value_gradient, preferred_element_type=jnp.float32)

    def spread(row_values):
        return jnp.zeros((SEQUENCE_LENGTH, row_values.shape[1]), jnp.bfloat16).at[kept_list].set(row_values)
    return ((spread(attended), spread(grad_rows), spread(grad_query), spread(key_gradient)), weight_term)

def reference(hidden, queries, rotary_keys, attn_cotangent, value_matrix, keep_index):

    def visit(total, items):
        seq_hidden, seq_queries, seq_keys, seq_cot, kept_list = items
        placed, weight_term = one_sequence(seq_hidden, seq_queries, seq_keys, seq_cot, value_matrix, kept_list)
        return (total + weight_term, placed)
    starting_total = jnp.zeros((MODEL_WIDTH, KEY_VALUE_HEADS * HEAD_SIZE), jnp.float32)
    total, placed = lax.scan(visit, starting_total, (hidden, queries, rotary_keys, attn_cotangent, keep_index))
    attn, grad_hidden, grad_queries, grad_keys = placed
    return (attn, grad_hidden, grad_queries, grad_keys, total.astype(jnp.bfloat16))
```

```python
import math

import jax
import jax.numpy as jnp
from jax import lax
from jax.experimental import pallas as pl
from jax.experimental.pallas import tpu as pltpu
from jax.sharding import PartitionSpec as P

WIDTH = 8192
HEAD = 128
HEADS = 32
GROUPS = 4
PER_GROUP = HEADS // GROUPS
KV = GROUPS * HEAD
TOK = 256
EVEN = 128
MARGIN = 32
SLOTS = EVEN + 2 * MARGIN
KEEP = 1024
PADDED = KEEP + 2 * MARGIN
SUB = 32
BLOCKS = SLOTS // SUB
LANES = SUB * PER_GROUP
SCALE = 1.0 / math.sqrt(HEAD)
LOG2E = math.log2(math.e)
BF = jnp.bfloat16
F32 = jnp.float32


CORE_SWAP = [(i, i ^ 1) for i in range(8)]
Z_UP = {k: [(i, i + 2 * k) for i in range(8 - 2 * k)] for k in (1, 2, 3)}
Z_DOWN = {k: [(t, s) for s, t in Z_UP[k]] for k in (1, 2, 3)}
Z_RING = {k: [(i, (i + 2 * k) % 8) for i in range(8)] for k in (1, 2, 3)}
X_RING = {k: [(i, (i + k) % 4) for i in range(4)] for k in (1, 2, 3)}
XY_TURN = {k: [(x * 4 + y, ((y + k) % 4) * 4 + x) for x in range(4) for y in range(4)] for k in range(4)}


def nt(a, b):
    return lax.dot_general(a, b, (((1,), (1,)), ((), ())), preferred_element_type=F32)


def nn(a, b):
    return jnp.dot(a, b, preferred_element_type=F32)


def owner_row(scal, rel, k):
    z, core = scal[0], scal[1]
    other = core + rel * (1 - 2 * core)
    return pl.multiple_of((jnp.maximum(z - k, 0) * 2 + other) * EVEN, EVEN)


def fill(scal, dst, own, partner):
    dst[...] = jnp.zeros_like(dst)
    for rel, part in ((0, own), (1, partner)):
        for k in range(4):
            at = owner_row(scal, rel, k)

            @pl.when(scal[0] >= k)
            def _():
                here = dst[pl.ds(at, SLOTS), :]
                dst[pl.ds(at, SLOTS), :] = here + part[k]


def windows(scal, out, acc, scale):
    for rel in range(2):
        for k in range(4):
            at = owner_row(scal, rel, k)

            @pl.when(scal[0] >= k)
            def _():
                out[rel, k] = (acc[pl.ds(at, SLOTS), :] * scale).astype(BF)

            @pl.when(scal[0] < k)
            def _():
                out[rel, k] = jnp.zeros((SLOTS, HEAD), BF)


def select_kernel(scal, slot_ref, hid_ref, out_ref):
    start, core = scal[2], scal[1]
    pos = lax.broadcasted_iota(jnp.int32, (SLOTS, TOK), 1) + start
    pick = jnp.where(slot_ref[...] == pos, 1.0, 0.0).astype(BF)
    rows = nn(pick, hid_ref[0]).astype(BF)
    for j in range(4):
        c = j % 2
        rel = c + core * (1 - 2 * c)
        out_ref[0, rel, :, (j // 2) * 256 : (j // 2 + 1) * 256] = rows[:, j * 256 : (j + 1) * 256]


def select_hidden(scal, slot_col, hidden):
    return pl.pallas_call(
        select_kernel,
        grid_spec=pltpu.PrefetchScalarGridSpec(
            num_scalar_prefetch=1,
            grid=(8,),
            in_specs=[
                pl.BlockSpec((SLOTS, 1), lambda i, s: (0, 0)),
                pl.BlockSpec((1, TOK, 1024), lambda i, s: (0, 0, i)),
            ],
            out_specs=pl.BlockSpec((1, 2, SLOTS, 512), lambda i, s: ((i // 2 - s[3]) & 3, 0, 0, i % 2)),
        ),
        out_shape=jax.ShapeDtypeStruct((4, 2, SLOTS, 1024), BF),
        name="select_hidden",
    )(scal, slot_col, hidden)


def probs_kernel(scal, slot_ref, q_ref, cot_ref, ko_ref, kp_ref, p_ref, qs_ref, cs_ref, k_ref, dv_ref, acc):
    start, base = scal[2], scal[4]
    pos = lax.broadcasted_iota(jnp.int32, (SLOTS, TOK), 1) + start
    pick = jnp.where(slot_ref[...] == pos, 1.0, 0.0).astype(BF)
    for src, dst in ((q_ref, qs_ref), (cot_ref, cs_ref)):
        rows = nn(pick, src[0]).astype(BF)
        for b in range(BLOCKS):
            for h in range(PER_GROUP):
                dst[0, b * LANES + h * SUB : b * LANES + (h + 1) * SUB, :] = rows[
                    b * SUB : (b + 1) * SUB, h * HEAD : (h + 1) * HEAD
                ]
    fill(scal, k_ref, ko_ref, kp_ref)
    acc[...] = jnp.zeros_like(acc)
    keys = k_ref[MARGIN : MARGIN + KEEP, :]
    key_id = lax.broadcasted_iota(jnp.int32, (KEEP, LANES), 0)
    lane_id = lax.broadcasted_iota(jnp.int32, (1, LANES), 1) & (SUB - 1)
    for b in range(BLOCKS):
        at = b * LANES
        s = nt(keys, qs_ref[0, at : at + LANES, :])
        s = jnp.where(key_id <= lane_id + (base + b * SUB), s, -1e30)
        top = jnp.max(s, axis=0, keepdims=True)
        e = jnp.exp2((s - top) * (SCALE * LOG2E))
        total = jnp.sum(e, axis=0, keepdims=True)
        p = (e * (1.0 / total)).astype(BF)
        p_ref[0, b] = p
        acc[MARGIN : MARGIN + KEEP, :] += nn(p, cs_ref[0, at : at + LANES, :])
    windows(scal, dv_ref, acc, 1.0)


def probs_call(scal, slot_col, queries, cot, k_own, k_partner):
    rows = pl.BlockSpec((1, TOK, 1024), lambda g, s: (0, 0, g))
    piece = pl.BlockSpec((4, SLOTS, HEAD), lambda g, s: (0, 0, g))
    stack = pl.BlockSpec((1, BLOCKS * LANES, HEAD), lambda g, s: (g, 0, 0))
    return pl.pallas_call(
        probs_kernel,
        grid_spec=pltpu.PrefetchScalarGridSpec(
            num_scalar_prefetch=1,
            grid=(GROUPS,),
            in_specs=[pl.BlockSpec((SLOTS, 1), lambda g, s: (0, 0)), rows, rows, piece, piece],
            out_specs=[
                pl.BlockSpec((1, BLOCKS, KEEP, LANES), lambda g, s: (g, 0, 0, 0)),
                stack,
                stack,
                pl.BlockSpec((PADDED, HEAD), lambda g, s: (0, g)),
                pl.BlockSpec((2, 4, SLOTS, HEAD), lambda g, s: (0, 0, 0, g)),
            ],
            scratch_shapes=[pltpu.VMEM((PADDED, HEAD), F32)],
        ),
        out_shape=[
            jax.ShapeDtypeStruct((GROUPS, BLOCKS, KEEP, LANES), BF),
            jax.ShapeDtypeStruct((GROUPS, BLOCKS * LANES, HEAD), BF),
            jax.ShapeDtypeStruct((GROUPS, BLOCKS * LANES, HEAD), BF),
            jax.ShapeDtypeStruct((PADDED, KV), BF),
            jax.ShapeDtypeStruct((2, 4, SLOTS, KV), BF),
        ],
        name="probs_and_value_grad",
    )(scal, slot_col, queries, cot, k_own, k_partner)


def grads_kernel(
    scal, slot_ref, p_ref, qs_ref, cs_ref, k_ref, vo_ref, vp_ref, at_ref, gq_ref, dk_ref, acc, v_scr, o_scr, g_scr
):
    start = scal[2]
    fill(scal, v_scr, vo_ref, vp_ref)
    acc[...] = jnp.zeros_like(acc)
    keys = k_ref[MARGIN : MARGIN + KEEP, :]
    vals = v_scr[MARGIN : MARGIN + KEEP, :]
    keys_t = keys.T
    vals_t = vals.T
    for b in range(BLOCKS):
        at = b * LANES
        p = p_ref[0, b]
        cot = cs_ref[0, at : at + LANES, :]
        out_t = nn(vals_t, p).astype(BF).astype(F32)
        cot_t = cot.astype(F32).T
        row_dot = jnp.sum(out_t * cot_t, axis=0, keepdims=True)
        ds = (p.astype(F32) * (nt(vals, cot) - row_dot)).astype(BF)
        gq_t = nn(keys_t, ds) * SCALE
        acc[MARGIN : MARGIN + KEEP, :] += nn(ds, qs_ref[0, at : at + LANES, :])
        out = out_t.T.astype(BF)
        gq = gq_t.T.astype(BF)
        for h in range(PER_GROUP):
            o_scr[b * SUB : (b + 1) * SUB, h * HEAD : (h + 1) * HEAD] = out[h * SUB : (h + 1) * SUB, :]
            g_scr[b * SUB : (b + 1) * SUB, h * HEAD : (h + 1) * HEAD] = gq[h * SUB : (h + 1) * SUB, :]
    pos = lax.broadcasted_iota(jnp.int32, (TOK, SLOTS), 0) + start
    place = jnp.where(slot_ref[...] == pos, 1.0, 0.0).astype(BF)
    at_ref[0] = nn(place, o_scr[...]).astype(BF)
    gq_ref[0] = nn(place, g_scr[...]).astype(BF)
    windows(scal, dk_ref, acc, SCALE)


def grads_call(scal, slot_row, probs, qs, cs, keys, v_own, v_partner):
    piece = pl.BlockSpec((4, SLOTS, HEAD), lambda g, s: (0, 0, g))
    stack = pl.BlockSpec((1, BLOCKS * LANES, HEAD), lambda g, s: (g, 0, 0))
    rows = pl.BlockSpec((1, TOK, 1024), lambda g, s: (0, 0, g))
    return pl.pallas_call(
        grads_kernel,
        grid_spec=pltpu.PrefetchScalarGridSpec(
            num_scalar_prefetch=1,
            grid=(GROUPS,),
            in_specs=[
                pl.BlockSpec((1, SLOTS), lambda g, s: (0, 0)),
                pl.BlockSpec((1, BLOCKS, KEEP, LANES), lambda g, s: (g, 0, 0, 0)),
                stack,
                stack,
                pl.BlockSpec((PADDED, HEAD), lambda g, s: (0, g)),
                piece,
                piece,
            ],
            out_specs=[rows, rows, pl.BlockSpec((2, 4, SLOTS, HEAD), lambda g, s: (0, 0, 0, g))],
            scratch_shapes=[
                pltpu.VMEM((PADDED, HEAD), F32),
                pltpu.VMEM((PADDED, HEAD), BF),
                pltpu.VMEM((SLOTS, PER_GROUP * HEAD), BF),
                pltpu.VMEM((SLOTS, PER_GROUP * HEAD), BF),
            ],
        ),
        out_shape=[
            jax.ShapeDtypeStruct((1, TOK, HEADS * HEAD), BF),
            jax.ShapeDtypeStruct((1, TOK, HEADS * HEAD), BF),
            jax.ShapeDtypeStruct((2, 4, SLOTS, KV), BF),
        ],
        name="attention_grads",
    )(scal, slot_row, probs, qs, cs, keys, v_own, v_partner)


def to_later(piece):
    got = [lax.ppermute(piece, "ctx", Z_UP[k]) for k in (1, 2, 3)]
    own = jnp.stack([piece] + got)
    return own, lax.ppermute(own, "ctx", CORE_SWAP)


def to_owner(parts):
    swapped = lax.ppermute(parts[1], "ctx", CORE_SWAP)
    both = (parts[0].astype(F32) + swapped.astype(F32)).astype(BF)
    got = [lax.ppermute(both[k], "ctx", Z_DOWN[k]) for k in (1, 2, 3)]
    total = both[0].astype(F32)
    for g in got:
        total = total + g.astype(F32)
    return total.astype(BF)


def local(hidden, queries, rotary_keys, attn_cotangent, value_matrix, keep_index):
    ctx = lax.axis_index("ctx")
    z, core, x = ctx // 2, ctx % 2, lax.axis_index("dp")
    start = ctx * TOK
    base = ctx * EVEN - MARGIN
    scal = jnp.stack([z, core, start, x, base]).astype(jnp.int32)
    fence = jnp.full((MARGIN,), -1, jnp.int32)
    padded = jnp.concatenate([fence, keep_index[0], fence])
    slot = lax.dynamic_slice(padded, (ctx * EVEN,), (SLOTS,))
    slot_col, slot_row = slot[:, None], slot[None, :]
    here = start + jnp.arange(TOK, dtype=jnp.int32)
    pick = (slot_col == here[None, :]).astype(BF)
    place = (slot_row == here[:, None]).astype(BF)

    whole = lax.all_gather(value_matrix, ("fsdp", "ctx"), axis=0, tiled=True)

    k_rows = nn(pick, rotary_keys[0]).astype(BF)
    k_own, k_partner = to_later(k_rows)

    pieces = select_hidden(scal, slot_col, hidden)
    from_x = [lax.ppermute(pieces[k], "dp", X_RING[k]) for k in (1, 2, 3)]
    mine = [pieces[0]] + from_x
    hid_partner = lax.ppermute(jnp.stack([m[1] for m in mine]), "ctx", CORE_SWAP)
    hid_own = jnp.stack([m[0] for m in mine])

    probs, qs, cs, keys, dv_parts = probs_call(scal, slot_col, queries, attn_cotangent, k_own, k_partner)
    grad_values = to_owner(dv_parts)

    v_pos = nn(hidden[0], whole).astype(BF)
    v_rows = nn(pick, v_pos).astype(BF)
    v_own, v_partner = to_later(v_rows)

    gv_pos = nn(place, grad_values).astype(BF)
    grad_hidden = nt(gv_pos, whole).astype(BF)

    gv_own = jnp.stack([grad_values] + [lax.ppermute(grad_values, "dp", X_RING[k]) for k in (1, 2, 3)])
    gv_partner = lax.ppermute(gv_own, "ctx", CORE_SWAP)
    tn = (((0,), (0,)), ((), ()))
    dw = lax.dot_general(
        jnp.concatenate([hid_own, hid_partner]).reshape(8 * SLOTS, 1024),
        jnp.concatenate([gv_own, gv_partner]).reshape(8 * SLOTS, KV),
        tn,
        preferred_element_type=F32,
    )
    dw = dw.astype(BF).reshape(4, 256, KV)
    total = lax.dynamic_index_in_dim(dw, z, keepdims=False).astype(F32)
    for k in (1, 2, 3):
        piece = lax.dynamic_index_in_dim(dw, (z + k) % 4, keepdims=False)
        total = total + lax.ppermute(piece, "ctx", Z_RING[k]).astype(F32)
    total = total.astype(BF)
    grad_weight = jnp.zeros((256, KV), F32)
    for k in range(4):
        grad_weight = grad_weight + lax.ppermute(total, ("dp", "fsdp"), XY_TURN[k]).astype(F32)
    grad_weight = grad_weight.astype(BF)

    attn, grad_queries, dk_parts = grads_call(scal, slot_row, probs, qs, cs, keys, v_own, v_partner)
    gk_rows = to_owner(dk_parts)
    grad_keys = nn(place, gk_rows).astype(BF)
    return (attn, grad_hidden[None], grad_queries, grad_keys[None], grad_weight)


def solution(mesh):
    rows = P(("dp", "fsdp"), "ctx", None)
    weight = P(("fsdp", "ctx"), None)
    return jax.shard_map(
        local,
        mesh=mesh,
        in_specs=(rows, rows, rows, rows, weight, P(("dp", "fsdp"), None)),
        out_specs=(rows, rows, rows, rows, weight),
        check_vma=False,
    )
```

```python
import math

import jax
import jax.numpy as jnp
from jax import lax
from jax.experimental import pallas as pl
from jax.experimental.pallas import tpu as pltpu
from jax.sharding import PartitionSpec as P


WIDTH = 8192
HEAD = 128
HEADS = 32
GROUPS = 4
PER_GROUP = HEADS // GROUPS
KV = GROUPS * HEAD
TOK = 256
EVEN = 128
MARGIN = 32
SLOTS = EVEN + 2 * MARGIN
KEEP = 1024
PADDED = KEEP + 2 * MARGIN
SUB = 32
BLOCKS = SLOTS // SUB
LANES = SUB * PER_GROUP
SCALE = 1.0 / math.sqrt(HEAD)
LOG2E = math.log2(math.e)
BF = jnp.bfloat16
F32 = jnp.float32


CORE_SWAP = [(i, i ^ 1) for i in range(8)]
Z_UP = {k: [(i, i + 2 * k) for i in range(8 - 2 * k)] for k in (1, 2, 3)}
Z_DOWN = {k: [(t, s) for s, t in Z_UP[k]] for k in (1, 2, 3)}
RING = {k: [(i, (i + k) % 4) for i in range(4)] for k in (1, 2, 3)}
XZ_TURN = {
    k: [
        (x * 8 + 2 * z + c, ((z + k) % 4) * 8 + 2 * x + c)
        for x in range(4)
        for z in range(4)
        for c in range(2)
    ]
    for k in range(4)
}


def nt(a, b):
    return lax.dot_general(a, b, (((1,), (1,)), ((), ())), preferred_element_type=F32)


def nn(a, b):
    return jnp.dot(a, b, preferred_element_type=F32)


def owner_row(scal, rel, k):
    z, core = scal[0], scal[1]
    other = core + rel * (1 - 2 * core)
    return pl.multiple_of((jnp.maximum(z - k, 0) * 2 + other) * EVEN, EVEN)


def fill(scal, dst, own, partner):
    dst[...] = jnp.zeros_like(dst)
    for rel, part in ((0, own), (1, partner)):
        for k in range(4):
            at = owner_row(scal, rel, k)

            @pl.when(scal[0] >= k)
            def _():
                here = dst[pl.ds(at, SLOTS), :]
                dst[pl.ds(at, SLOTS), :] = here + part[k]


def windows(scal, outs, acc, scale):
    for rel in range(2):
        for k in range(4):
            at = owner_row(scal, rel, k)

            @pl.when(scal[0] >= k)
            def _():
                outs[rel][k] = (acc[pl.ds(at, SLOTS), :] * scale).astype(BF)

            @pl.when(scal[0] < k)
            def _():
                outs[rel][k] = jnp.zeros((SLOTS, HEAD), BF)


def select_kernel(scal, slot_ref, hid_ref, out_ref):
    pos = lax.broadcasted_iota(jnp.int32, (SLOTS, TOK), 1) + scal[2]
    pick = jnp.where(slot_ref[...] == pos, 1.0, 0.0).astype(BF)
    for y in range(2):
        for z in range(4):
            at = y * 2048 + z * 512
            out_ref[z, :, y * 512 : (y + 1) * 512] = nn(pick, hid_ref[0, :, at : at + 512]).astype(BF)


def select_hidden(scal, slot_col, hidden):
    return pl.pallas_call(
        select_kernel,
        grid_spec=pltpu.PrefetchScalarGridSpec(
            num_scalar_prefetch=1,
            grid=(2,),
            in_specs=[
                pl.BlockSpec((SLOTS, 1), lambda i, s: (0, 0)),
                pl.BlockSpec((1, TOK, 4096), lambda i, s: (0, 0, i)),
            ],
            out_specs=pl.BlockSpec((4, SLOTS, 1024), lambda i, s: (0, 0, i)),
        ),
        out_shape=jax.ShapeDtypeStruct((4, SLOTS, 2048), BF),
        name="select_hidden",
    )(scal, slot_col, hidden)


def values_kernel(hid_ref, w_ref, out_ref, acc):
    @pl.when(pl.program_id(0) == 0)
    def _():
        acc[...] = jnp.zeros_like(acc)

    total = acc[...]
    for z in range(4):
        total = total + nn(hid_ref[z], w_ref[z * 512 : (z + 1) * 512, :])
    acc[...] = total
    out_ref[...] = total.astype(BF)


def values_call(pieces, weight):
    return pl.pallas_call(
        values_kernel,
        grid=(4,),
        in_specs=[
            pl.BlockSpec((4, SLOTS, 512), lambda i: (0, 0, i)),
            pl.BlockSpec((2048, KV), lambda i: (i, 0)),
        ],
        out_specs=pl.BlockSpec((SLOTS, KV), lambda i: (0, 0)),
        out_shape=jax.ShapeDtypeStruct((SLOTS, KV), BF),
        scratch_shapes=[pltpu.VMEM((SLOTS, KV), F32)],
        name="values",
    )(pieces, weight)


def weight_kernel(scal, h0, h1, h2, h3, g0, g1, g2, g3, own_ref, other_ref, acc):
    total = None
    for h, g in ((h0, g0), (h1, g1), (h2, g2), (h3, g3)):
        term = lax.dot_general(h[0], g[...], (((0,), (0,)), ((), ())), preferred_element_type=F32)
        total = term if total is None else total + term
    acc[...] = total
    own_ref[0] = acc[pl.ds(pl.multiple_of(scal[1] * 256, 256), 256), :].astype(BF)
    other_ref[0] = acc[pl.ds(pl.multiple_of((1 - scal[1]) * 256, 256), 256), :].astype(BF)


def weight_call(scal, hid, grad):
    cols = [pl.BlockSpec((1, SLOTS, 512), lambda i, s, k=k: ((s[3] - k) & 3, 0, i)) for k in range(4)]
    rows = pl.BlockSpec((SLOTS, KV), lambda i, s: (0, 0))
    out = pl.BlockSpec((1, 256, KV), lambda i, s: ((i - s[5]) & 3, 0, 0))
    return pl.pallas_call(
        weight_kernel,
        grid_spec=pltpu.PrefetchScalarGridSpec(
            num_scalar_prefetch=1,
            grid=(4,),
            in_specs=cols + [rows] * 4,
            out_specs=[out, out],
            scratch_shapes=[pltpu.VMEM((512, KV), F32)],
        ),
        out_shape=[jax.ShapeDtypeStruct((4, 256, KV), BF)] * 2,
        name="weight_terms",
    )(scal, hid, hid, hid, hid, *grad)


def hidden_grad_kernel(gv_ref, w_ref, out_ref):
    out_ref[0] = nt(gv_ref[...], w_ref[...]).astype(BF)


def hidden_grad(gv_pos, weight):
    return pl.pallas_call(
        hidden_grad_kernel,
        grid=(4,),
        in_specs=[pl.BlockSpec((TOK, KV), lambda i: (0, 0)), pl.BlockSpec((2048, KV), lambda i: (i, 0))],
        out_specs=pl.BlockSpec((1, TOK, 2048), lambda i: (0, 0, i)),
        out_shape=jax.ShapeDtypeStruct((1, TOK, WIDTH), BF),
        name="hidden_grad",
    )(gv_pos, weight)


def probs_kernel(scal, slot_ref, q_ref, cot_ref, ko_ref, kp_ref, p_ref, qs_ref, cs_ref, k_ref, dv0_ref, dv1_ref, acc):
    start, base = scal[2], scal[4]
    pos = lax.broadcasted_iota(jnp.int32, (SLOTS, TOK), 1) + start
    pick = jnp.where(slot_ref[...] == pos, 1.0, 0.0).astype(BF)
    for src, dst in ((q_ref, qs_ref), (cot_ref, cs_ref)):
        rows = nn(pick, src[0]).astype(BF)
        for b in range(BLOCKS):
            for h in range(PER_GROUP):
                dst[0, b * LANES + h * SUB : b * LANES + (h + 1) * SUB, :] = rows[
                    b * SUB : (b + 1) * SUB, h * HEAD : (h + 1) * HEAD
                ]
    fill(scal, k_ref, ko_ref, kp_ref)
    acc[...] = jnp.zeros_like(acc)
    keys = k_ref[MARGIN : MARGIN + KEEP, :]
    key_id = lax.broadcasted_iota(jnp.int32, (KEEP, LANES), 0)
    lane_id = lax.broadcasted_iota(jnp.int32, (1, LANES), 1) & (SUB - 1)

    def scores(b):
        return nt(keys, qs_ref[0, b * LANES : (b + 1) * LANES, :])

    ahead = scores(0)
    for b in range(BLOCKS):
        at = b * LANES
        s = ahead
        if b + 1 < BLOCKS:
            ahead = scores(b + 1)
        s = jnp.where(key_id <= lane_id + (base + b * SUB), s, -1e30)
        top = jnp.max(s, axis=0, keepdims=True)
        e = jnp.exp2((s - top) * (SCALE * LOG2E))
        total = jnp.sum(e, axis=0, keepdims=True)
        p = (e * (1.0 / total)).astype(BF)
        p_ref[0, b] = p
        acc[MARGIN : MARGIN + KEEP, :] += nn(p, cs_ref[0, at : at + LANES, :])
    windows(scal, (dv0_ref, dv1_ref), acc, 1.0)


def probs_call(scal, slot_col, queries, cot, k_own, k_partner):
    rows = pl.BlockSpec((1, TOK, 1024), lambda g, s: (0, 0, g))
    piece = pl.BlockSpec((4, SLOTS, HEAD), lambda g, s: (0, 0, g))
    stack = pl.BlockSpec((1, BLOCKS * LANES, HEAD), lambda g, s: (g, 0, 0))
    return pl.pallas_call(
        probs_kernel,
        grid_spec=pltpu.PrefetchScalarGridSpec(
            num_scalar_prefetch=1,
            grid=(GROUPS,),
            in_specs=[pl.BlockSpec((SLOTS, 1), lambda g, s: (0, 0)), rows, rows, piece, piece],
            out_specs=[
                pl.BlockSpec((1, BLOCKS, KEEP, LANES), lambda g, s: (g, 0, 0, 0)),
                stack,
                stack,
                pl.BlockSpec((PADDED, HEAD), lambda g, s: (0, g)),
                piece,
                piece,
            ],
            scratch_shapes=[pltpu.VMEM((PADDED, HEAD), F32)],
        ),
        out_shape=[
            jax.ShapeDtypeStruct((GROUPS, BLOCKS, KEEP, LANES), BF),
            jax.ShapeDtypeStruct((GROUPS, BLOCKS * LANES, HEAD), BF),
            jax.ShapeDtypeStruct((GROUPS, BLOCKS * LANES, HEAD), BF),
            jax.ShapeDtypeStruct((PADDED, KV), BF),
            jax.ShapeDtypeStruct((4, SLOTS, KV), BF),
            jax.ShapeDtypeStruct((4, SLOTS, KV), BF),
        ],
        name="probs_and_value_grad",
    )(scal, slot_col, queries, cot, k_own, k_partner)


def grads_kernel(scal, slot_ref, p_ref, qs_ref, cs_ref, k_ref, vo_ref, vp_ref, *rest):
    at_ref, gq_ref, dk0_ref, dk1_ref, acc, v_scr, o_scr, g_scr = rest[-8:]
    start = scal[2]
    fill(scal, v_scr, vo_ref, vp_ref)
    acc[...] = jnp.zeros_like(acc)
    keys = k_ref[MARGIN : MARGIN + KEEP, :]
    vals = v_scr[MARGIN : MARGIN + KEEP, :]
    keys_t = keys.T
    vals_t = vals.T
    for b in range(BLOCKS):
        at = b * LANES
        p = p_ref[0, b]
        cot = cs_ref[0, at : at + LANES, :]
        out_t = nn(vals_t, p).astype(BF).astype(F32)
        cot_t = cot.astype(F32).T
        row_dot = jnp.sum(out_t * cot_t, axis=0, keepdims=True)
        ds = (p.astype(F32) * (nt(vals, cot) - row_dot)).astype(BF)
        gq_t = nn(keys_t, ds) * SCALE
        acc[MARGIN : MARGIN + KEEP, :] += nn(ds, qs_ref[0, at : at + LANES, :])
        out = out_t.T.astype(BF)
        gq = gq_t.T.astype(BF)
        for h in range(PER_GROUP):
            o_scr[b * SUB : (b + 1) * SUB, h * HEAD : (h + 1) * HEAD] = out[h * SUB : (h + 1) * SUB, :]
            g_scr[b * SUB : (b + 1) * SUB, h * HEAD : (h + 1) * HEAD] = gq[h * SUB : (h + 1) * SUB, :]
    pos = lax.broadcasted_iota(jnp.int32, (TOK, SLOTS), 0) + start
    place = jnp.where(slot_ref[...] == pos, 1.0, 0.0).astype(BF)
    at_ref[0] = nn(place, o_scr[...]).astype(BF)
    gq_ref[0] = nn(place, g_scr[...]).astype(BF)
    windows(scal, (dk0_ref, dk1_ref), acc, SCALE)


def grads_call(scal, slot_row, probs, qs, cs, keys, v_own, v_partner):
    piece = pl.BlockSpec((4, SLOTS, HEAD), lambda g, s: (0, 0, g))
    stack = pl.BlockSpec((1, BLOCKS * LANES, HEAD), lambda g, s: (g, 0, 0))
    rows = pl.BlockSpec((1, TOK, 1024), lambda g, s: (0, 0, g))
    whole = jax.ShapeDtypeStruct((1, TOK, HEADS * HEAD), BF)
    terms = jax.ShapeDtypeStruct((4, SLOTS, KV), BF)
    return pl.pallas_call(
        grads_kernel,
        grid_spec=pltpu.PrefetchScalarGridSpec(
            num_scalar_prefetch=1,
            grid=(GROUPS,),
            in_specs=[
                pl.BlockSpec((1, SLOTS), lambda g, s: (0, 0)),
                pl.BlockSpec((1, BLOCKS, KEEP, LANES), lambda g, s: (g, 0, 0, 0)),
                stack,
                stack,
                pl.BlockSpec((PADDED, HEAD), lambda g, s: (0, g)),
                piece,
                piece,
            ],
            out_specs=[rows, rows, piece, piece],
            scratch_shapes=[
                pltpu.VMEM((PADDED, HEAD), F32),
                pltpu.VMEM((PADDED, HEAD), BF),
                pltpu.VMEM((SLOTS, PER_GROUP * HEAD), BF),
                pltpu.VMEM((SLOTS, PER_GROUP * HEAD), BF),
            ],
        ),
        out_shape=[whole, whole, terms, terms],
        name="attention_grads",
    )(scal, slot_row, probs, qs, cs, keys, v_own, v_partner)


def to_later(piece, beside=()):
    got = [lax.ppermute(piece, "ctx", Z_UP[k]) for k in (2, 1, 3)]
    own = jnp.stack([piece, got[1], got[0], got[2]])
    if beside:
        own, *beside = lax.optimization_barrier((own, *beside))
    partner = lax.ppermute(own, "ctx", CORE_SWAP)
    return own, partner, beside


def to_owner(same, other, after=None):
    swapped = lax.ppermute(other, "ctx", CORE_SWAP)
    both = [(same[k].astype(F32) + swapped[k].astype(F32)).astype(BF) for k in range(4)]
    got = [both[0]] + [lax.ppermute(both[k], "ctx", Z_DOWN[k]) for k in (2, 1, 3)]
    if after is not None:
        got = lax.optimization_barrier((after, *got))[1:]
    return sum(g.astype(F32) for g in got).astype(BF), both[0]


def local(hidden, queries, rotary_keys, attn_cotangent, value_matrix, keep_index):
    ctx = lax.axis_index("ctx")
    z, core = ctx // 2, ctx % 2
    start = ctx * TOK
    base = ctx * EVEN - MARGIN
    scal = jnp.stack([z, core, start, lax.axis_index("dp"), base, lax.axis_index("fsdp")]).astype(jnp.int32)
    fence = jnp.full((MARGIN,), -1, jnp.int32)
    padded = jnp.concatenate([fence, keep_index[0], fence])
    slot = lax.dynamic_slice(padded, (ctx * EVEN,), (SLOTS,))
    slot_col, slot_row = slot[:, None], slot[None, :]
    here = start + jnp.arange(TOK, dtype=jnp.int32)
    pick = (slot_col == here[None, :]).astype(BF)
    place = (slot_row == here[:, None]).astype(BF)

    weight = lax.all_gather(value_matrix, ("fsdp", "ctx"), axis=0, tiled=True)

    k_rows = nn(pick, rotary_keys[0]).astype(BF)
    pieces = select_hidden(scal, slot_col, hidden)
    k_own, k_partner, (pieces,) = to_later(k_rows, (pieces,))
    hid = lax.all_to_all(pieces, "dp", 0, 0, tiled=True)

    probs, qs, cs, keys, dv_same, dv_other = probs_call(
        scal, slot_col, queries, attn_cotangent, k_own, k_partner
    )

    v_rows = values_call(pieces, weight)
    grad_values, _ = to_owner(dv_same, dv_other, v_rows)
    v_own, v_partner, _ = to_later(v_rows)

    gv = [grad_values] + [lax.ppermute(grad_values, "dp", RING[k]) for k in (1, 2, 3)]
    dw_same, dw_other = weight_call(scal, hid, gv)
    swapped = lax.ppermute(dw_other, "ctx", CORE_SWAP)
    both = [dw_same[k].astype(F32) + swapped[k].astype(F32) for k in range(4)]
    total = both[0]
    both = [b.astype(BF) for b in both]
    got = [lax.ppermute(both[k], "fsdp", RING[k]) for k in (2, 1, 3)]

    attn, gq, dk_same, dk_other = grads_call(scal, slot_row, probs, qs, cs, keys, v_own, v_partner)
    gk_rows, dk_first = to_owner(dk_same, dk_other)

    got = lax.optimization_barrier((dk_first, *got))[1:]
    total = sum((g.astype(F32) for g in got), total).astype(BF)
    got = [lax.ppermute(total, ("dp", "ctx"), XZ_TURN[k]) for k in range(4)]
    grad_weight = sum(g.astype(F32) for g in got).astype(BF)

    gv_late, dk_other = lax.optimization_barrier((grad_values, dk_other))
    grad_hidden = hidden_grad(nn(place, gv_late).astype(BF), weight)
    grad_keys = nn(place, gk_rows).astype(BF)
    return (attn, grad_hidden, gq, grad_keys[None], grad_weight)


def solution(mesh):
    rows = P(("dp", "fsdp"), "ctx", None)
    weight = P(("fsdp", "ctx"), None)

    return jax.shard_map(
        local,
        mesh=mesh,
        in_specs=(rows, rows, rows, rows, weight, P(("dp", "fsdp"), None)),
        out_specs=(rows, rows, rows, rows, weight),
        check_vma=False,
    )
```

```python
import math

import jax
import jax.numpy as jnp
from jax import lax
from jax.experimental import pallas as pl
from jax.experimental.pallas import tpu as pltpu
from jax.sharding import PartitionSpec as P


WIDTH = 8192
HEAD = 128
HEADS = 32
GROUPS = 4
PER_GROUP = HEADS // GROUPS
KV = GROUPS * HEAD
TOK = 256
EVEN = 128
MARGIN = 32
SLOTS = EVEN + 2 * MARGIN
KEEP = 1024
PADDED = KEEP + 2 * MARGIN
SUB = 32
BLOCKS = SLOTS // SUB
LANES = SUB * PER_GROUP
SCALE = 1.0 / math.sqrt(HEAD)
LOG2E = math.log2(math.e)
BF = jnp.bfloat16
F32 = jnp.float32


CORE_SWAP = [(i, i ^ 1) for i in range(8)]
Z_UP = {k: [(i, i + 2 * k) for i in range(8 - 2 * k)] for k in (1, 2, 3)}
Z_DOWN = {k: [(t, s) for s, t in Z_UP[k]] for k in (1, 2, 3)}
RING = {k: [(i, (i + k) % 4) for i in range(4)] for k in (1, 2, 3)}
XZ_TURN = {
    k: [
        (x * 8 + 2 * z + c, ((z + k) % 4) * 8 + 2 * x + c)
        for x in range(4)
        for z in range(4)
        for c in range(2)
    ]
    for k in range(4)
}


def nt(a, b):
    return lax.dot_general(a, b, (((1,), (1,)), ((), ())), preferred_element_type=F32)


def nn(a, b):
    return jnp.dot(a, b, preferred_element_type=F32)


def owner_row(scal, rel, k):
    z, core = scal[0], scal[1]
    other = core + rel * (1 - 2 * core)
    return pl.multiple_of((jnp.maximum(z - k, 0) * 2 + other) * EVEN, EVEN)


def fill(scal, dst, own, partner):
    dst[...] = jnp.zeros_like(dst)
    for rel, part in ((0, own), (1, partner)):
        for k in range(4):
            at = owner_row(scal, rel, k)

            @pl.when(scal[0] >= k)
            def _():
                here = dst[pl.ds(at, SLOTS), :]
                dst[pl.ds(at, SLOTS), :] = here + part[k]


def windows(scal, outs, acc, scale):
    for rel in range(2):
        for k in range(4):
            at = owner_row(scal, rel, k)

            @pl.when(scal[0] >= k)
            def _():
                outs[rel][k] = (acc[pl.ds(at, SLOTS), :] * scale).astype(BF)

            @pl.when(scal[0] < k)
            def _():
                outs[rel][k] = jnp.zeros((SLOTS, HEAD), BF)


def select_kernel(scal, slot_ref, hid_ref, out_ref):
    pos = lax.broadcasted_iota(jnp.int32, (SLOTS, TOK), 1) + scal[2]
    pick = jnp.where(slot_ref[...] == pos, 1.0, 0.0).astype(BF)
    for y in range(2):
        for z in range(4):
            at = y * 2048 + z * 512
            out_ref[z, :, y * 512 : (y + 1) * 512] = nn(pick, hid_ref[0, :, at : at + 512]).astype(BF)


def select_hidden(scal, slot_col, hidden):
    return pl.pallas_call(
        select_kernel,
        grid_spec=pltpu.PrefetchScalarGridSpec(
            num_scalar_prefetch=1,
            grid=(2,),
            in_specs=[
                pl.BlockSpec((SLOTS, 1), lambda i, s: (0, 0)),
                pl.BlockSpec((1, TOK, 4096), lambda i, s: (0, 0, i)),
            ],
            out_specs=pl.BlockSpec((4, SLOTS, 1024), lambda i, s: (0, 0, i)),
        ),
        out_shape=jax.ShapeDtypeStruct((4, SLOTS, 2048), BF),
        name="select_hidden",
    )(scal, slot_col, hidden)


def values_kernel(hid_ref, w_ref, out_ref, acc):
    @pl.when(pl.program_id(0) == 0)
    def _():
        acc[...] = jnp.zeros_like(acc)

    total = acc[...]
    for z in range(4):
        total = total + nn(hid_ref[z], w_ref[z * 512 : (z + 1) * 512, :])
    acc[...] = total
    out_ref[...] = total.astype(BF)


def values_call(pieces, weight):
    return pl.pallas_call(
        values_kernel,
        grid=(4,),
        in_specs=[
            pl.BlockSpec((4, SLOTS, 512), lambda i: (0, 0, i)),
            pl.BlockSpec((2048, KV), lambda i: (i, 0)),
        ],
        out_specs=pl.BlockSpec((SLOTS, KV), lambda i: (0, 0)),
        out_shape=jax.ShapeDtypeStruct((SLOTS, KV), BF),
        scratch_shapes=[pltpu.VMEM((SLOTS, KV), F32)],
        name="values",
    )(pieces, weight)


def weight_kernel(scal, h0, h1, h2, h3, g0, g1, g2, g3, own_ref, other_ref, acc):
    total = None
    for h, g in ((h0, g0), (h1, g1), (h2, g2), (h3, g3)):
        term = lax.dot_general(h[0], g[...], (((0,), (0,)), ((), ())), preferred_element_type=F32)
        total = term if total is None else total + term
    acc[...] = total
    own_ref[0] = acc[pl.ds(pl.multiple_of(scal[1] * 256, 256), 256), :].astype(BF)
    other_ref[0] = acc[pl.ds(pl.multiple_of((1 - scal[1]) * 256, 256), 256), :].astype(BF)


def weight_call(scal, hid, grad):
    cols = [pl.BlockSpec((1, SLOTS, 512), lambda i, s, k=k: ((s[3] - k) & 3, 0, i)) for k in range(4)]
    rows = pl.BlockSpec((SLOTS, KV), lambda i, s: (0, 0))
    out = pl.BlockSpec((1, 256, KV), lambda i, s: ((i - s[5]) & 3, 0, 0))
    return pl.pallas_call(
        weight_kernel,
        grid_spec=pltpu.PrefetchScalarGridSpec(
            num_scalar_prefetch=1,
            grid=(4,),
            in_specs=cols + [rows] * 4,
            out_specs=[out, out],
            scratch_shapes=[pltpu.VMEM((512, KV), F32)],
        ),
        out_shape=[jax.ShapeDtypeStruct((4, 256, KV), BF)] * 2,
        name="weight_terms",
    )(scal, hid, hid, hid, hid, *grad)


def hidden_grad_kernel(gv_ref, w_ref, out_ref):
    out_ref[0] = nt(gv_ref[...], w_ref[...]).astype(BF)


def hidden_grad(gv_pos, weight):
    return pl.pallas_call(
        hidden_grad_kernel,
        grid=(4,),
        in_specs=[pl.BlockSpec((TOK, KV), lambda i: (0, 0)), pl.BlockSpec((2048, KV), lambda i: (i, 0))],
        out_specs=pl.BlockSpec((1, TOK, 2048), lambda i: (0, 0, i)),
        out_shape=jax.ShapeDtypeStruct((1, TOK, WIDTH), BF),
        name="hidden_grad",
    )(gv_pos, weight)


def probs_kernel(scal, slot_ref, q_ref, cot_ref, ko_ref, kp_ref, p_ref, qs_ref, cs_ref, k_ref, dv0_ref, dv1_ref, acc):
    start, base = scal[2], scal[4]
    pos = lax.broadcasted_iota(jnp.int32, (SLOTS, TOK), 1) + start
    pick = jnp.where(slot_ref[...] == pos, 1.0, 0.0).astype(BF)
    for src, dst in ((q_ref, qs_ref), (cot_ref, cs_ref)):
        rows = nn(pick, src[0]).astype(BF)
        for b in range(BLOCKS):
            for h in range(PER_GROUP):
                dst[0, b * LANES + h * SUB : b * LANES + (h + 1) * SUB, :] = rows[
                    b * SUB : (b + 1) * SUB, h * HEAD : (h + 1) * HEAD
                ]
    fill(scal, k_ref, ko_ref, kp_ref)
    acc[...] = jnp.zeros_like(acc)
    keys = k_ref[MARGIN : MARGIN + KEEP, :]
    key_id = lax.broadcasted_iota(jnp.int32, (KEEP, LANES), 0)
    lane_id = lax.broadcasted_iota(jnp.int32, (1, LANES), 1) & (SUB - 1)

    def scores(b):
        return nt(keys, qs_ref[0, b * LANES : (b + 1) * LANES, :])

    ahead = scores(0)
    for b in range(BLOCKS):
        at = b * LANES
        s = ahead
        if b + 1 < BLOCKS:
            ahead = scores(b + 1)
        s = jnp.where(key_id <= lane_id + (base + b * SUB), s, -1e30)
        top = jnp.max(s, axis=0, keepdims=True)
        e = jnp.exp2((s - top) * (SCALE * LOG2E))
        total = jnp.sum(e, axis=0, keepdims=True)
        p = (e * (1.0 / total)).astype(BF)
        p_ref[0, b] = p
        acc[MARGIN : MARGIN + KEEP, :] += nn(p, cs_ref[0, at : at + LANES, :])
    windows(scal, (dv0_ref, dv1_ref), acc, 1.0)


def probs_call(scal, slot_col, queries, cot, k_own, k_partner):
    rows = pl.BlockSpec((1, TOK, 1024), lambda g, s: (0, 0, g))
    piece = pl.BlockSpec((4, SLOTS, HEAD), lambda g, s: (0, 0, g))
    stack = pl.BlockSpec((1, BLOCKS * LANES, HEAD), lambda g, s: (g, 0, 0))
    return pl.pallas_call(
        probs_kernel,
        grid_spec=pltpu.PrefetchScalarGridSpec(
            num_scalar_prefetch=1,
            grid=(GROUPS,),
            in_specs=[pl.BlockSpec((SLOTS, 1), lambda g, s: (0, 0)), rows, rows, piece, piece],
            out_specs=[
                pl.BlockSpec((1, BLOCKS, KEEP, LANES), lambda g, s: (g, 0, 0, 0)),
                stack,
                stack,
                pl.BlockSpec((PADDED, HEAD), lambda g, s: (0, g)),
                piece,
                piece,
            ],
            scratch_shapes=[pltpu.VMEM((PADDED, HEAD), F32)],
        ),
        out_shape=[
            jax.ShapeDtypeStruct((GROUPS, BLOCKS, KEEP, LANES), BF),
            jax.ShapeDtypeStruct((GROUPS, BLOCKS * LANES, HEAD), BF),
            jax.ShapeDtypeStruct((GROUPS, BLOCKS * LANES, HEAD), BF),
            jax.ShapeDtypeStruct((PADDED, KV), BF),
            jax.ShapeDtypeStruct((4, SLOTS, KV), BF),
            jax.ShapeDtypeStruct((4, SLOTS, KV), BF),
        ],
        name="probs_and_value_grad",
    )(scal, slot_col, queries, cot, k_own, k_partner)


def grads_kernel(scal, slot_ref, p_ref, qs_ref, cs_ref, k_ref, v_ref, *rest):
    at_ref, gq_ref, dk0_ref, dk1_ref, acc, v_scr, o_scr, g_scr = rest[-8:]
    start = scal[2]
    v_scr[...] = jnp.zeros_like(v_scr)
    for i in range(8):
        v_scr[i * EVEN : i * EVEN + SLOTS, :] += v_ref[i]
    acc[...] = jnp.zeros_like(acc)
    keys = k_ref[MARGIN : MARGIN + KEEP, :]
    vals = v_scr[MARGIN : MARGIN + KEEP, :]
    keys_t = keys.T
    vals_t = vals.T
    for b in range(BLOCKS):
        at = b * LANES
        p = p_ref[0, b]
        cot = cs_ref[0, at : at + LANES, :]
        out_t = nn(vals_t, p).astype(BF).astype(F32)
        cot_t = cot.astype(F32).T
        row_dot = jnp.sum(out_t * cot_t, axis=0, keepdims=True)
        ds = (p.astype(F32) * (nt(vals, cot) - row_dot)).astype(BF)
        gq_t = nn(keys_t, ds) * SCALE
        acc[MARGIN : MARGIN + KEEP, :] += nn(ds, qs_ref[0, at : at + LANES, :])
        out = out_t.T.astype(BF)
        gq = gq_t.T.astype(BF)
        for h in range(PER_GROUP):
            o_scr[b * SUB : (b + 1) * SUB, h * HEAD : (h + 1) * HEAD] = out[h * SUB : (h + 1) * SUB, :]
            g_scr[b * SUB : (b + 1) * SUB, h * HEAD : (h + 1) * HEAD] = gq[h * SUB : (h + 1) * SUB, :]
    pos = lax.broadcasted_iota(jnp.int32, (TOK, SLOTS), 0) + start
    place = jnp.where(slot_ref[...] == pos, 1.0, 0.0).astype(BF)
    at_ref[0] = nn(place, o_scr[...]).astype(BF)
    gq_ref[0] = nn(place, g_scr[...]).astype(BF)
    windows(scal, (dk0_ref, dk1_ref), acc, SCALE)


def grads_call(scal, slot_row, probs, qs, cs, keys, every_v):
    piece = pl.BlockSpec((4, SLOTS, HEAD), lambda g, s: (0, 0, g))
    stack = pl.BlockSpec((1, BLOCKS * LANES, HEAD), lambda g, s: (g, 0, 0))
    rows = pl.BlockSpec((1, TOK, 1024), lambda g, s: (0, 0, g))
    whole = jax.ShapeDtypeStruct((1, TOK, HEADS * HEAD), BF)
    terms = jax.ShapeDtypeStruct((4, SLOTS, KV), BF)
    return pl.pallas_call(
        grads_kernel,
        grid_spec=pltpu.PrefetchScalarGridSpec(
            num_scalar_prefetch=1,
            grid=(GROUPS,),
            in_specs=[
                pl.BlockSpec((1, SLOTS), lambda g, s: (0, 0)),
                pl.BlockSpec((1, BLOCKS, KEEP, LANES), lambda g, s: (g, 0, 0, 0)),
                stack,
                stack,
                pl.BlockSpec((PADDED, HEAD), lambda g, s: (0, g)),
                pl.BlockSpec((8, SLOTS, HEAD), lambda g, s: (0, 0, g)),
            ],
            out_specs=[rows, rows, piece, piece],
            scratch_shapes=[
                pltpu.VMEM((PADDED, HEAD), F32),
                pltpu.VMEM((PADDED, HEAD), BF),
                pltpu.VMEM((SLOTS, PER_GROUP * HEAD), BF),
                pltpu.VMEM((SLOTS, PER_GROUP * HEAD), BF),
            ],
        ),
        out_shape=[whole, whole, terms, terms],
        name="attention_grads",
    )(scal, slot_row, probs, qs, cs, keys, every_v)


def to_later(piece, beside=()):
    got = [lax.ppermute(piece, "ctx", Z_UP[k]) for k in (2, 1, 3)]
    own = jnp.stack([piece, got[1], got[0], got[2]])
    if beside:
        own, *beside = lax.optimization_barrier((own, *beside))
    partner = lax.ppermute(own, "ctx", CORE_SWAP)
    return own, partner, beside


def to_owner(same, other, after=None):
    swapped = lax.ppermute(other, "ctx", CORE_SWAP)
    both = [(same[k].astype(F32) + swapped[k].astype(F32)).astype(BF) for k in range(4)]
    got = [both[0]] + [lax.ppermute(both[k], "ctx", Z_DOWN[k]) for k in (2, 1, 3)]
    if after is not None:
        got = lax.optimization_barrier((after, *got))[1:]
    return sum(g.astype(F32) for g in got).astype(BF), both[0]


def local(hidden, queries, rotary_keys, attn_cotangent, value_matrix, keep_index):
    ctx = lax.axis_index("ctx")
    z, core = ctx // 2, ctx % 2
    start = ctx * TOK
    base = ctx * EVEN - MARGIN
    scal = jnp.stack([z, core, start, lax.axis_index("dp"), base, lax.axis_index("fsdp")]).astype(jnp.int32)
    fence = jnp.full((MARGIN,), -1, jnp.int32)
    padded = jnp.concatenate([fence, keep_index[0], fence])
    slot = lax.dynamic_slice(padded, (ctx * EVEN,), (SLOTS,))
    slot_col, slot_row = slot[:, None], slot[None, :]
    here = start + jnp.arange(TOK, dtype=jnp.int32)
    pick = (slot_col == here[None, :]).astype(BF)
    place = (slot_row == here[:, None]).astype(BF)

    weight = lax.all_gather(value_matrix, ("fsdp", "ctx"), axis=0, tiled=True)

    k_rows = nn(pick, rotary_keys[0]).astype(BF)
    pieces = select_hidden(scal, slot_col, hidden)
    k_own, k_partner, (pieces,) = to_later(k_rows, (pieces,))
    hid = lax.all_to_all(pieces, "dp", 0, 0, tiled=True)

    probs, qs, cs, keys, dv_same, dv_other = probs_call(
        scal, slot_col, queries, attn_cotangent, k_own, k_partner
    )

    v_rows = values_call(pieces, weight)
    grad_values, _ = to_owner(dv_same, dv_other, v_rows)
    every_v = lax.all_gather(v_rows, "ctx", axis=0, tiled=False)

    gv = [grad_values] + [lax.ppermute(grad_values, "dp", RING[k]) for k in (1, 2, 3)]
    dw_same, dw_other = weight_call(scal, hid, gv)
    swapped = lax.ppermute(dw_other, "ctx", CORE_SWAP)
    both = [dw_same[k].astype(F32) + swapped[k].astype(F32) for k in range(4)]
    total = both[0]
    both = [b.astype(BF) for b in both]
    got = [lax.ppermute(both[k], "fsdp", RING[k]) for k in (2, 1, 3)]

    attn, gq, dk_same, dk_other = grads_call(scal, slot_row, probs, qs, cs, keys, every_v)
    gk_rows, dk_first = to_owner(dk_same, dk_other)

    got = lax.optimization_barrier((dk_first, *got))[1:]
    total = sum((g.astype(F32) for g in got), total).astype(BF)
    got = [lax.ppermute(total, ("dp", "ctx"), XZ_TURN[k]) for k in range(4)]
    grad_weight = sum(g.astype(F32) for g in got).astype(BF)

    grad_hidden = hidden_grad(nn(place, grad_values).astype(BF), weight)
    grad_keys = nn(place, gk_rows).astype(BF)
    return (attn, grad_hidden, gq, grad_keys[None], grad_weight)


def solution(mesh):
    rows = P(("dp", "fsdp"), "ctx", None)
    weight = P(("fsdp", "ctx"), None)

    return jax.shard_map(
        local,
        mesh=mesh,
        in_specs=(rows, rows, rows, rows, weight, P(("dp", "fsdp"), None)),
        out_specs=(rows, rows, rows, rows, weight),
        check_vma=False,
    )
```
